256 devices in a mesh: dp: 2 (over core), row: 16 (over x, y), col: 8 (over z).
Axes of the slice: x: 4, y: 4, z: 8, core: 2. Of those that a mesh axis runs over, the one named last changes fastest.
Arguments:
- tokens: bfloat16 [768, 8192], P(('dp', 'col'), 'row'), may hold values from -160 to 160
- norm_gain: float32 [8192], P('row'), may hold values from 0.3 to 3
- gate_weight: bfloat16 [8192, 14336], P('row', ('dp', 'col')), may hold values from -0.0625 to 0.0625
- up_weight: bfloat16 [8192, 14336], P('row', ('dp', 'col')), may hold values from -0.0625 to 0.0625
- down_weight: bfloat16 [14336, 8192], P(('dp', 'col'), 'row'), may hold values from -0.046875 to 0.046875
- gate_keep: int32 [64, 112], P('row', ('dp', 'col')), may hold values from 0 to 1, as said below
- up_keep: int32 [64, 112], P('row', ('dp', 'col')), may hold values from 0 to 1, as said below
- down_keep: int32 [112, 64], P(('dp', 'col'), 'row'), may hold values from 0 to 1, as said below
- cotangent: bfloat16 [768, 8192], P(('dp', 'col'), 'row'), may hold values from -80 to 80
Outputs:
- branch: bfloat16 [768, 8192], P(('dp', 'col'), 'row')
- grad_tokens: float32 [768, 8192], P(('dp', 'col'), 'row')
- grad_gain: float32 [8192], P('row')
- grad_gate: float32 [8192, 14336], P('row', ('dp', 'col'))
- grad_up: float32 [8192, 14336], P('row', ('dp', 'col'))
- grad_down: float32 [14336, 8192], P(('dp', 'col'), 'row')
The draws below stay inside these ranges and needn't reach their ends.
Inputs may be any that keep to these rules, and one draw needn't show every extreme that they name: `gate_keep`: 1 keeps a 128 x 128 block of the gate projection, 0 prunes it. `up_keep`: 1 keeps a 128 x 128 block of the up projection, 0 prunes it. `down_keep`: 1 keeps a 128 x 128 block of the down projection, 0 prunes it.
All inputs are finite; a program needn't handle non-finite values.
Results may differ from the reference program's by a relative error of at most 0.0065.
Values may be sent and summed in bfloat16 or wider, within the bound.
A program may use at most 128 MiB of HBM per device.

```python
import math
import jax
import jax.numpy as jnp
from jax import lax

D = 8192
FF = 14336
BLOCK = 128
TOKENS = 768


def keep_levels(key, salt, rows, cols, along_rows):
    level_key = jax.random.fold_in(key, salt)
    roll_key = jax.random.fold_in(key, salt + 1)
    if along_rows:
        level = jax.random.randint(level_key, (rows, 1), 1, 8)
    else:
        level = jax.random.randint(level_key, (1, cols), 1, 8)
    roll = jax.random.randint(roll_key, (rows, cols), 0, 8)
    return (roll < level).astype(jnp.int32)


def draw_gate_keep(key, part):
    return keep_levels(key, 101, D // BLOCK, FF // BLOCK, True)


def draw_up_keep(key, part):
    return keep_levels(key, 203, D // BLOCK, FF // BLOCK, True)


def draw_down_keep(key, part):
    return keep_levels(key, 307, FF // BLOCK, D // BLOCK, False)


def scaled_field(key, salt, col_ramp, row_ramp, col_hi, row_lo, row_hi):
    keys = [jax.random.fold_in(key, salt + step) for step in range(4)]
    col_factor = jnp.exp(jax.random.uniform(keys[0], (1, D), jnp.float32, 0.0, math.log(col_hi)))
    row_factor = jnp.exp(jax.random.uniform(keys[1], (TOKENS, 1), jnp.float32, math.log(row_lo), math.log(row_hi)))
    base = jnp.clip(jax.random.normal(keys[2], (TOKENS, D), jnp.float32), -4.0, 4.0)
    return base * col_factor * row_factor * col_ramp * row_ramp


def draw_tokens(key, part):
    col_ramp = 3.0 ** (jnp.arange(D, dtype=jnp.float32)[None, :] / D)
    row_ramp = jnp.ones((TOKENS, 1), jnp.float32)
    return scaled_field(key, 401, col_ramp, row_ramp, 3.3, 0.4, 4.0).astype(jnp.bfloat16)


def draw_cotangent(key, part):
    col_ramp = jnp.ones((1, D), jnp.float32)
    row_ramp = 3.0 ** (jnp.arange(TOKENS, dtype=jnp.float32)[:, None] / TOKENS)
    return scaled_field(key, 503, col_ramp, row_ramp, 2.0, 1.0, 3.3).astype(jnp.bfloat16)


def block_levels(rng, shape, cuts, low, high):
    level, own = 1.0, jax.random.fold_in(rng, 6)
    for axis_at, shards_of in cuts:
        draws = jnp.exp(jax.random.uniform(jax.random.fold_in(own, axis_at), (shards_of,), jnp.float32, low / len(cuts), high / len(cuts)))
        level = level * jnp.repeat(draws, shape[axis_at] // shards_of).reshape([-1 if axis == axis_at else 1 for axis in range(len(shape))])
    return level


def centred(key, extent, deviation, reach, cuts=(), held_as=jnp.bfloat16):
    loudness = block_levels(key, extent, cuts, -0.22, 0.18) if cuts else 1.0
    result = jax.random.normal(key, extent, jnp.float32) * deviation * loudness
    return jnp.minimum(jnp.maximum(result, -reach), reach).astype(held_as)


def setup_inputs(seed: int = 0) -> dict:
    arg_keys = jax.random.split(jax.random.key(seed), 10)
    return {
        "tokens": draw_tokens(jax.random.fold_in(arg_keys[9], 71), 0),
        "norm_gain": jnp.clip(jnp.exp(math.log(3.0) - 2.3025851 * jax.random.uniform(arg_keys[1], (D,), jnp.float32) ** block_levels(arg_keys[1], (D,), ((0, 16),), -0.2, 0.2)), 0.3, 3.0),
        "gate_weight": centred(arg_keys[2], (D, FF), D ** -0.5, 0.0625, ((0, 16), (1, 16))),
        "up_weight": centred(arg_keys[3], (D, FF), D ** -0.5, 0.0625, ((0, 16), (1, 16))),
        "down_weight": centred(arg_keys[4], (FF, D), FF ** -0.5, 0.046875, ((0, 16), (1, 16))),
        "gate_keep": draw_gate_keep(jax.random.fold_in(arg_keys[9], 71), 0),
        "up_keep": draw_up_keep(jax.random.fold_in(arg_keys[9], 71), 0),
        "down_keep": draw_down_keep(jax.random.fold_in(arg_keys[9], 71), 0),
        "cotangent": draw_cotangent(jax.random.fold_in(arg_keys[9], 71), 0),
    }


def expand_keep(keep, target_type):
    return jnp.repeat(jnp.repeat(keep, BLOCK, axis=0), BLOCK, axis=1).astype(target_type)

def reference(tokens, norm_gain, gate_weight, up_weight, down_weight, gate_keep, up_keep, down_keep, cotangent):
    token_f = tokens.astype(jnp.float32)
    inv_rms = lax.rsqrt(lax.optimization_barrier(jnp.mean(token_f * token_f, axis=1, keepdims=True)) + 1e-05)
    normed = (token_f * inv_rms * norm_gain).astype(jnp.bfloat16)
    gate_masked = gate_weight * expand_keep(gate_keep, jnp.bfloat16)
    up_masked = up_weight * expand_keep(up_keep, jnp.bfloat16)
    down_masked = down_weight * expand_keep(down_keep, jnp.bfloat16)
    gate = jnp.dot(normed, gate_masked, preferred_element_type=jnp.float32)
    up_value = jnp.dot(normed, up_masked, preferred_element_type=jnp.float32)
    sigmoid_gate = jax.nn.sigmoid(gate)
    hidden = (gate * sigmoid_gate * up_value).astype(jnp.bfloat16)
    branch = jnp.dot(hidden, down_masked, preferred_element_type=jnp.float32).astype(jnp.bfloat16)
    hidden_grad = jnp.dot(cotangent, down_masked.T, preferred_element_type=jnp.float32)
    gate_grad = (hidden_grad * up_value * sigmoid_gate * (1.0 + gate * (1.0 - sigmoid_gate))).astype(jnp.bfloat16)
    up_grad = (hidden_grad * gate * sigmoid_gate).astype(jnp.bfloat16)
    grad_down = jnp.dot(hidden.T, cotangent, preferred_element_type=jnp.float32) * expand_keep(down_keep, jnp.float32)
    grad_gate = jnp.dot(normed.T, gate_grad, preferred_element_type=jnp.float32) * expand_keep(gate_keep, jnp.float32)
    grad_up = jnp.dot(normed.T, up_grad, preferred_element_type=jnp.float32) * expand_keep(up_keep, jnp.float32)
    normed_grad = jnp.dot(gate_grad, gate_masked.T, preferred_element_type=jnp.float32) + jnp.dot(up_grad, up_masked.T, preferred_element_type=jnp.float32)
    grad_gain = lax.optimization_barrier(jnp.sum(normed_grad * token_f * inv_rms, axis=0))
    inner_dot = lax.optimization_barrier(jnp.sum(norm_gain * normed_grad * token_f, axis=1, keepdims=True))
    grad_tokens = inv_rms * norm_gain * normed_grad - token_f * inv_rms * inv_rms * inv_rms * inner_dot / D
    return (branch, grad_tokens, grad_gain, grad_gate, grad_up, grad_down)
```

```python
import jax
import jax.numpy as jnp
from jax import lax
from jax.experimental import pallas as pl
from jax.experimental.pallas import tpu as pltpu
from jax.sharding import PartitionSpec as P

D = 8192
BLOCK = 128
T = 48
W = 512
U = 896
F32 = jnp.float32
BF16 = jnp.bfloat16
MESH = pl.DeviceIdType.MESH
VM = pl.BlockSpec(memory_space=pltpu.VMEM)
VMEM_LIMIT = 48 * 1024 * 1024


def rcopy(src, dst, send, recv, dev):
    return pltpu.make_async_remote_copy(
        src_ref=src, dst_ref=dst, send_sem=send, recv_sem=recv, device_id=dev, device_id_type=MESH
    )


def greet(devices):
    barrier = pltpu.get_barrier_semaphore()
    for dev in devices:
        pl.semaphore_signal(barrier, inc=1, device_id=dev, device_id_type=MESH)
    pl.semaphore_wait(barrier, len(devices))


def add(*values):
    total = values[0].astype(F32)
    for value in values[1:]:
        total = total + value.astype(F32)
    return total


def peers_of_row(row):
    return [{"row": lax.rem(row + k, 16)} for k in range(1, 16)]


def peers_of_cols(dp, z):
    me = dp * 8 + z
    found = []
    for k in range(1, 16):
        other = lax.rem(me + k, 16)
        found.append({"dp": other // 8, "col": lax.rem(other, 8)})
    return found


def gather_kernel(
    tok, cot, squares, x_out, c_out, inv_out, sq_buf,
    ring_send, ring_recv, pair_send, pair_recv, sq_send, sq_recv, inv_send, inv_recv,
):
    dp, row, z = lax.axis_index("dp"), lax.axis_index("row"), lax.axis_index("col")
    row_peers = peers_of_row(row)
    col_peers = peers_of_cols(dp, z)
    right, left = {"col": lax.rem(z + 1, 8)}, {"col": lax.rem(z + 7, 8)}
    mate = {"dp": 1 - dp}
    x_out[dp, z] = tok[...]
    c_out[dp, z] = cot[...]
    sq_buf[row] = squares[...]
    greet(row_peers + col_peers)
    outs = (x_out, c_out)
    started = []

    def begin(copy):
        copy.start()
        started.append(copy)
        return copy

    squared = [
        begin(rcopy(squares, sq_buf.at[row], sq_send.at[k], sq_recv.at[k], row_peers[k]))
        for k in range(15)
    ]

    def ring(side, step, unit):
        block = lax.rem(z + (9 - step if side == 0 else step + 7), 8)
        here = (tok, cot)[unit] if step == 1 else outs[unit].at[dp, block]
        return begin(
            rcopy(
                here, outs[unit].at[dp, block],
                ring_send.at[side, step - 1, unit], ring_recv.at[side, step - 1, unit],
                right if side == 0 else left,
            )
        )

    def pair(slot, block, unit, own=False):
        here = (tok, cot)[unit] if own else outs[unit].at[dp, block]
        begin(rcopy(here, outs[unit].at[dp, block], pair_send.at[slot, unit], pair_recv.at[slot, unit], mate))

    flying = {}
    for unit in range(2):
        for side in range(2):
            u = unit if side == 0 else 1 - unit
            flying[side, 1, u] = ring(side, 1, u)
    for unit in range(2):
        pair(0, z, unit, own=True)

    inv_done = []
    for step in range(1, 5):
        for unit in range(2):
            for side in range(2):
                u = unit if side == 0 else 1 - unit
                if step == 4 and u != side:
                    continue
                flying[side, step, u].wait_recv()
                if step < 3 or (step == 3 and u == side):
                    flying[side, step + 1, u] = ring(side, step + 1, u)
                block = lax.rem(z + (8 - step if side == 0 else step), 8)
                slot = step if side == 0 or step == 4 else step + 4
                pair(slot, block, u)
        if step == 1:
            for copy in squared:
                copy.wait_recv()
            total = sq_buf[0]
            for k in range(1, 16):
                total = total + sq_buf[k]
            inv_out[dp * 8 + z] = lax.rsqrt(total / D + 1e-05)
            inv_done = [
                begin(
                    rcopy(
                        inv_out.at[dp * 8 + z], inv_out.at[dp * 8 + z],
                        inv_send.at[k], inv_recv.at[k], col_peers[k],
                    )
                )
                for k in range(15)
            ]
    for slot in range(8):
        for unit in range(2):
            rcopy(
                tok, x_out.at[1 - dp, z], pair_send.at[slot, unit], pair_recv.at[slot, unit], mate
            ).wait_recv()
    for copy in inv_done:
        copy.wait_recv()
    for copy in started:
        copy.wait_send()


def gather(tok, cot, squares):
    return pl.pallas_call(
        gather_kernel,
        out_shape=(
            jax.ShapeDtypeStruct((2, 8, T, W), BF16),
            jax.ShapeDtypeStruct((2, 8, T, W), BF16),
            jax.ShapeDtypeStruct((16, 1, 128), F32),
        ),
        in_specs=[VM] * 3,
        out_specs=(VM,) * 3,
        scratch_shapes=[
            pltpu.VMEM((16, 1, 128), F32),
            pltpu.SemaphoreType.DMA((2, 4, 2)),
            pltpu.SemaphoreType.DMA((2, 4, 2)),
            pltpu.SemaphoreType.DMA((8, 2)),
            pltpu.SemaphoreType.DMA((8, 2)),
            pltpu.SemaphoreType.DMA((15,)),
            pltpu.SemaphoreType.DMA((15,)),
            pltpu.SemaphoreType.DMA((15,)),
            pltpu.SemaphoreType.DMA((15,)),
        ],
        compiler_params=pltpu.CompilerParams(
            collective_id=0, has_side_effects=True, vmem_limit_bytes=VMEM_LIMIT
        ),
        name="gather_tokens",
    )(tok, cot, squares)


LANES = 3 * U
PARTS = (((0, 768), (768, 640)), ((1408, 640), (2048, 640)))


class Ring:
    def __init__(self, pos, right, left):
        self.here = pos
        self.next = lax.rem(pos + 1, 4)
        self.far = lax.rem(pos + 2, 4)
        self.prev = lax.rem(pos + 3, 4)
        self.right, self.left = right, left


class Scatter:
    def __init__(self, ring, src, bufs, send, recv, started):
        self.ring, self.src, self.bufs = ring, src, bufs
        self.send, self.recv, self.started = send, recv, started
        self.copies = {}

    def go(self, k, src, dst, dev):
        copy = rcopy(src, dst, self.send.at[k], self.recv.at[k], dev)
        copy.start()
        self.started.append(copy)
        self.copies[k] = copy

    def begin(self):
        ring, src, b = self.ring, self.src, self.bufs
        self.go(0, src(ring.far, 0), b["hop"][0], ring.right)
        self.go(1, src(ring.far, 1), b["hop"][1], ring.left)
        self.go(2, src(ring.next, 1), b["left"][1], ring.right)
        self.go(3, src(ring.prev, 0), b["right"][0], ring.left)

    def middle(self, part):
        ring, src, b = self.ring, self.src, self.bufs
        self.copies[part].wait_recv()
        piece = src(ring.next if part == 0 else ring.prev, part)
        b["sum"][part][...] = add(piece[...], b["hop"][part][...]).astype(BF16)
        if part == 0:
            self.go(4, b["sum"][0], b["left"][0], ring.right)
        else:
            self.go(5, b["sum"][1], b["right"][1], ring.left)

    def end(self, part):
        b = self.bufs
        for k in ((3, 4), (2, 5))[part]:
            self.copies[k].wait_recv()
        own = self.src(self.ring.here, part)
        return add(own[...], b["left"][part][...], b["right"][part][...])


class Spread:
    def __init__(self, ring, slot, send, recv, started):
        self.ring, self.slot = ring, slot
        self.send, self.recv, self.started = send, recv, started
        self.copies = {}

    def go(self, k, ref, dev):
        copy = rcopy(ref, ref, self.send.at[k], self.recv.at[k], dev)
        copy.start()
        self.started.append(copy)
        self.copies[k] = copy

    def begin(self):
        ring, slot = self.ring, self.slot
        self.go(0, slot(ring.here, 0), ring.right)
        self.go(1, slot(ring.here, 1), ring.left)
        self.go(2, slot(ring.here, 1), ring.right)
        self.go(3, slot(ring.here, 0), ring.left)

    def middle(self, part):
        ring, slot = self.ring, self.slot
        self.copies[part].wait_recv()
        if part == 0:
            self.go(4, slot(ring.prev, 0), ring.right)
        else:
            self.go(5, slot(ring.next, 1), ring.left)

    def end(self):
        for k in range(2, 6):
            self.copies[k].wait_recv()


def activation(gate, up_value, hidden_grad):
    s = jax.nn.sigmoid(gate)
    hidden = (gate * s * up_value).astype(BF16)
    gate_grad = (hidden_grad * up_value * s * (1.0 + gate * (1.0 - s))).astype(BF16)
    up_grad = (hidden_grad * gate * s).astype(BF16)
    return hidden, gate_grad, up_grad


def exchange_kernel(p, q, *scratch):
    n = 0

    def take(count):
        nonlocal n
        n += count
        return scratch[n - count : n]

    big, small = [], []
    for store in (big, small):
        for chain in range(2):
            store.append({name: take(2) for name in ("hop", "sum", "left", "right")})
    mid = [take(2), take(2)]
    (total,) = take(1)
    send, recv = take(2)
    row = lax.axis_index("row")
    px, py = row // 4, lax.rem(row, 4)

    def at(x, y):
        return {"row": x * 4 + y}

    rings = (
        Ring(px, at(lax.rem(px + 1, 4), py), at(lax.rem(px + 3, 4), py)),
        Ring(py, at(px, lax.rem(py + 1, 4)), at(px, lax.rem(py + 3, 4))),
    )
    greet([rings[0].right, rings[0].left, rings[1].right, rings[1].left])
    started = []

    def lanes(chain, part):
        start, size = PARTS[chain][part]
        return pl.ds(start, size)

    def first_piece(ref, chain):
        if chain == 0:
            return lambda d, part: ref.at[d, :, :, lanes(chain, part)]
        return lambda d, part: ref.at[:, d, :, lanes(chain, part)]

    stage1 = [
        Scatter(rings[c], first_piece(p, c), big[c], send.at[c, 0], recv.at[c, 0], started) for c in range(2)
    ]
    for part in range(1):
        for c in range(2):
            stage1[c].begin()
    for part in range(2):
        for c in range(2):
            stage1[c].middle(part)
    stage2 = []
    for c in range(2):
        for part in range(2):
            mid[c][part][...] = stage1[c].end(part).astype(BF16)
        stage2.append(
            Scatter(
                rings[1 - c], lambda d, part, c=c: mid[c][part].at[d], small[c],
                send.at[c, 1], recv.at[c, 1], started,
            )
        )
        stage2[c].begin()
    for c in range(2):
        for part in range(2):
            stage2[c].middle(part)
    for c in range(2):
        for part in range(2):
            total[:, lanes(c, part)] = stage2[c].end(part)
    hidden, gate_grad, up_grad = activation(
        total[:, pl.ds(0, U)], total[:, pl.ds(U, U)], total[:, pl.ds(2 * U, U)]
    )
    q[px, py, :, pl.ds(0, U)] = hidden
    q[px, py, :, pl.ds(U, U)] = gate_grad
    q[px, py, :, pl.ds(2 * U, U)] = up_grad

    def near(c):
        if c == 0:
            return lambda d, part: q.at[px, d, :, lanes(c, part)]
        return lambda d, part: q.at[d, py, :, lanes(c, part)]

    stage3 = [Spread(rings[1 - c], near(c), send.at[c, 2], recv.at[c, 2], started) for c in range(2)]
    stage4 = [Spread(rings[c], first_piece(q, c), send.at[c, 3], recv.at[c, 3], started) for c in range(2)]
    for c in range(2):
        stage3[c].begin()
    for part in range(2):
        for c in range(2):
            stage3[c].middle(part)
    for c in range(2):
        stage3[c].end()
        stage4[c].begin()
    for part in range(2):
        for c in range(2):
            stage4[c].middle(part)
    for c in range(2):
        stage4[c].end()
    for copy in started:
        copy.wait_send()


def exchange(partials):
    scratch = []
    for lead in ((4, T), (T,)):
        for chain in range(2):
            for _ in range(4):
                for part in range(2):
                    scratch.append(pltpu.VMEM(lead + (PARTS[chain][part][1],), BF16))
    for chain in range(2):
        for part in range(2):
            scratch.append(pltpu.VMEM((4, T, PARTS[chain][part][1]), BF16))
    scratch.append(pltpu.VMEM((T, LANES), F32))
    scratch += [pltpu.SemaphoreType.DMA((2, 4, 6))] * 2
    return pl.pallas_call(
        exchange_kernel,
        out_shape=jax.ShapeDtypeStruct((4, 4, T, LANES), BF16),
        in_specs=[VM],
        out_specs=VM,
        scratch_shapes=scratch,
        compiler_params=pltpu.CompilerParams(
            collective_id=1, has_side_effects=True, vmem_limit_bytes=VMEM_LIMIT
        ),
        name="exchange_hidden",
    )(partials)


def finish_kernel(
    branch_part, grad_part, tok, inv, gain, branch_out, tokens_out, gain_out,
    pair_buf, go_buf, come_buf, square_buf, dot_buf, gain_buf,
    pair_send, pair_recv, ring_send, ring_recv, dot_send, dot_recv, gain_send, gain_recv,
):
    dp, row, z = lax.axis_index("dp"), lax.axis_index("row"), lax.axis_index("col")
    row_peers = peers_of_row(row)
    col_peers = peers_of_cols(dp, z)
    right, left = {"col": lax.rem(z + 1, 8)}, {"col": lax.rem(z + 7, 8)}
    mate = {"dp": 1 - dp}
    parts = (branch_part, grad_part)
    greet(row_peers + col_peers)
    started = []

    def begin(copy):
        copy.start()
        started.append(copy)
        return copy

    offsets = (4, 3, 5, 2, 6, 1, 7, 0)
    paired = {}
    for off in offsets:
        dest = lax.rem(z + off, 8)
        for unit in range(2):
            paired[off, unit] = begin(
                rcopy(
                    parts[unit].at[1 - dp, dest], pair_buf.at[unit, off],
                    pair_send.at[unit, off], pair_recv.at[unit, off], mate,
                )
            )
    known = set()

    def mine(off, unit):
        if (off, unit) not in known:
            paired[off, unit].wait_recv()
            known.add((off, unit))
        return add(parts[unit][dp, lax.rem(z + off, 8)], pair_buf[unit, off])

    ring = {}
    for step in range(1, 5):
        for unit in range(2):
            for side in range(2):
                u = unit if side == 0 else 1 - unit
                if step == 1 and u != side:
                    continue
                off = 5 - step if side == 0 else 3 + step
                value = mine(off, u)
                if step > 2 or (step == 2 and u == side):
                    ring[side, step - 1, u].wait_recv()
                    value = value + come_buf[side, step - 2, u].astype(F32)
                go_buf[side, step - 1, u] = value.astype(BF16)
                ring[side, step, u] = begin(
                    rcopy(
                        go_buf.at[side, step - 1, u], come_buf.at[side, step - 1, u],
                        ring_send.at[side, step - 1, u], ring_recv.at[side, step - 1, u],
                        right if side == 0 else left,
                    )
                )
    totals = []
    for unit in range(2):
        value = mine(0, unit)
        for side in range(2):
            ring[side, 4, unit].wait_recv()
            value = value + come_buf[side, 3, unit].astype(F32)
        totals.append(value)
    branch_out[...] = totals[0].astype(BF16)
    normed_grad = totals[1]
    token_f = tok[...].astype(F32)
    inv_rms = inv[:, 0:1]
    weighted = normed_grad * token_f
    gain_buf[dp * 8 + z] = jnp.sum(weighted * inv_rms, axis=0, keepdims=True)
    square_buf[...] = jnp.zeros((128, 128), F32)
    square_buf[pl.ds(0, T), :] = jnp.broadcast_to(
        jnp.sum(gain[...] * weighted, axis=1, keepdims=True), (T, 128)
    )
    dot_buf[row] = jnp.transpose(square_buf[...])[0:1]
    small = []
    for k in range(15):
        small.append(
            begin(rcopy(dot_buf.at[row], dot_buf.at[row], dot_send.at[k], dot_recv.at[k], row_peers[k]))
        )
        mine_at = gain_buf.at[dp * 8 + z]
        small.append(begin(rcopy(mine_at, mine_at, gain_send.at[k], gain_recv.at[k], col_peers[k])))
    for copy in small:
        copy.wait_recv()
    inner, gain_total = dot_buf[0], gain_buf[0]
    for k in range(1, 16):
        inner = inner + dot_buf[k]
        gain_total = gain_total + gain_buf[k]
    gain_out[...] = gain_total
    square_buf[...] = jnp.transpose(jnp.broadcast_to(inner, (128, 128)))
    inner_col = square_buf[pl.ds(0, T), 0:1]
    tokens_out[...] = inv_rms * gain[...] * normed_grad - token_f * inv_rms * inv_rms * inv_rms * inner_col / D
    for copy in started:
        copy.wait_send()


def finish(branch_part, grad_part, tok, inv, gain):
    return pl.pallas_call(
        finish_kernel,
        out_shape=(
            jax.ShapeDtypeStruct((T, W), BF16),
            jax.ShapeDtypeStruct((T, W), F32),
            jax.ShapeDtypeStruct((1, W), F32),
        ),
        in_specs=[VM] * 5,
        out_specs=(VM,) * 3,
        scratch_shapes=[
            pltpu.VMEM((2, 8, T, W), BF16),
            pltpu.VMEM((2, 4, 2, T, W), BF16),
            pltpu.VMEM((2, 4, 2, T, W), BF16),
            pltpu.VMEM((128, 128), F32),
            pltpu.VMEM((16, 1, 128), F32),
            pltpu.VMEM((16, 1, W), F32),
            pltpu.SemaphoreType.DMA((2, 8)),
            pltpu.SemaphoreType.DMA((2, 8)),
            pltpu.SemaphoreType.DMA((2, 4, 2)),
            pltpu.SemaphoreType.DMA((2, 4, 2)),
            pltpu.SemaphoreType.DMA((15,)),
            pltpu.SemaphoreType.DMA((15,)),
            pltpu.SemaphoreType.DMA((15,)),
            pltpu.SemaphoreType.DMA((15,)),
        ],
        compiler_params=pltpu.CompilerParams(
            collective_id=2, has_side_effects=True, vmem_limit_bytes=VMEM_LIMIT
        ),
        name="finish_tokens",
    )(branch_part, grad_part, tok, inv, gain)


def expand_keep(keep, target_type):
    return jnp.repeat(jnp.repeat(keep, BLOCK, axis=0), BLOCK, axis=1).astype(target_type)


LAST = (((1,), (1,)), ((), ()))
FIRST = (((0,), (0,)), ((), ()))


def on_device(
    tokens, norm_gain, gate_weight, up_weight, down_weight, gate_keep, up_keep, down_keep, cotangent
):
    gain = norm_gain[None, :]
    token_f = tokens.astype(F32)
    squares = jnp.pad(jnp.sum(token_f * token_f, axis=1), (0, 128 - T))[None, :]
    seen, cot, inv = gather(tokens, cotangent, squares)
    seen, cot = seen.reshape(16 * T, W), cot.reshape(16 * T, W)
    inv_all = inv[:, 0, :T].reshape(16 * T, 1)
    normed = (seen.astype(F32) * inv_all * gain).astype(BF16)
    keep_gu = jnp.concatenate([expand_keep(gate_keep, BF16), expand_keep(up_keep, BF16)], axis=1)
    gu_masked = jnp.concatenate([gate_weight, up_weight], axis=1) * keep_gu
    down_masked = down_weight * expand_keep(down_keep, BF16)
    gate_up = jnp.dot(normed, gu_masked, preferred_element_type=F32).astype(BF16)
    hidden_grad = lax.dot_general(cot, down_masked, LAST, preferred_element_type=F32).astype(BF16)
    partials = jnp.concatenate([gate_up, hidden_grad], axis=1).reshape(4, 4, T, LANES)
    shared = exchange(partials).reshape(16 * T, LANES)
    hidden, gu_grad = shared[:, :U], shared[:, U:]
    branch_part = jnp.dot(hidden, down_masked, preferred_element_type=F32).astype(BF16)
    grad_part = lax.dot_general(gu_grad, gu_masked, LAST, preferred_element_type=F32).astype(BF16)
    index = lax.axis_index("dp") * 8 + lax.axis_index("col")
    inv_own = jnp.broadcast_to(inv[index, 0, :T][:, None], (T, 128))
    branch, grad_tokens, grad_gain = finish(
        branch_part.reshape(2, 8, T, W), grad_part.reshape(2, 8, T, W), tokens, inv_own, gain
    )
    grad_gate = lax.dot_general(normed, gu_grad[:, :U], FIRST, preferred_element_type=F32)
    grad_up = lax.dot_general(normed, gu_grad[:, U:], FIRST, preferred_element_type=F32)
    grad_down = lax.dot_general(hidden, cot, FIRST, preferred_element_type=F32)
    return (
        branch,
        grad_tokens,
        grad_gain[0],
        grad_gate * expand_keep(gate_keep, F32),
        grad_up * expand_keep(up_keep, F32),
        grad_down * expand_keep(down_keep, F32),
    )


def solution(mesh):
    wide = P("row", ("dp", "col"))
    tall = P(("dp", "col"), "row")
    return jax.shard_map(
        on_device,
        mesh=mesh,
        in_specs=(tall, P("row"), wide, wide, tall, wide, wide, tall, tall),
        out_specs=(tall, tall, P("row"), wide, wide, tall),
        check_vma=False,
    )
```

```python
import jax
import jax.numpy as jnp
from jax import lax
from jax.experimental import pallas as pl
from jax.experimental.pallas import tpu as pltpu
from jax.sharding import PartitionSpec as P

D = 8192
T = 48
W = 512
U = 896
LANES = 3 * U
CHUNKS = ((0, 16), (16, 16), (32, 16))
SKEW = 2
F32 = jnp.float32
BF16 = jnp.bfloat16
MESH = pl.DeviceIdType.MESH
VM = pl.BlockSpec(memory_space=pltpu.VMEM)
SM = pl.BlockSpec(memory_space=pltpu.SMEM)
LAST = (((1,), (1,)), ((), ()))
FIRST = (((0,), (0,)), ((), ()))
PARTS = (((0, 768), (768, 640)), ((1408, 640), (2048, 640)))


def add(*values):
    total = values[0].astype(F32)
    for value in values[1:]:
        total = total + value.astype(F32)
    return total


def peers_of_row(row):
    return [{"row": lax.rem(row + k, 16)} for k in range(1, 16)]


def peers_of_cols(dp, z):
    me = dp * 8 + z
    found = []
    for k in range(1, 16):
        other = lax.rem(me + k, 16)
        found.append({"dp": other // 8, "col": lax.rem(other, 8)})
    return found


def greet(devices):
    barrier = pltpu.get_barrier_semaphore()
    for dev in devices:
        pl.semaphore_signal(barrier, inc=1, device_id=dev, device_id_type=MESH)
    pl.semaphore_wait(barrier, len(devices))


class Sender:
    def __init__(self):
        self.started = []

    def go(self, src, dst, send, recv, dev):
        copy = pltpu.make_async_remote_copy(
            src_ref=src, dst_ref=dst, send_sem=send, recv_sem=recv, device_id=dev, device_id_type=MESH
        )
        copy.start()
        self.started.append(copy)
        return copy

    def drain(self):
        for copy in self.started:
            copy.wait_send()


class Ring:
    def __init__(self, pos, right, left):
        self.here = pos
        self.next = lax.rem(pos + 1, 4)
        self.far = lax.rem(pos + 2, 4)
        self.prev = lax.rem(pos + 3, 4)
        self.right, self.left = right, left


class Scatter:
    def __init__(self, ring, wire, exact, bufs, send, recv, out):
        self.ring, self.wire, self.exact, self.bufs = ring, wire, exact, bufs
        self.send, self.recv, self.out = send, recv, out
        self.copies = {}

    def go(self, k, src, dst, dev):
        self.copies[k] = self.out.go(src, dst, self.send.at[k], self.recv.at[k], dev)

    def begin(self):
        ring, wire, b = self.ring, self.wire, self.bufs
        self.go(0, wire(ring.far, 0), b["hop"][0], ring.right)
        self.go(1, wire(ring.far, 1), b["hop"][1], ring.left)
        self.go(2, wire(ring.next, 1), b["left"][1], ring.right)
        self.go(3, wire(ring.prev, 0), b["right"][0], ring.left)

    def middle(self, part):
        ring, b = self.ring, self.bufs
        self.copies[part].wait_recv()
        piece = self.exact(ring.next if part == 0 else ring.prev, part)
        b["sum"][part][...] = add(piece[...], b["hop"][part][...]).astype(BF16)
        if part == 0:
            self.go(4, b["sum"][0], b["left"][0], ring.right)
        else:
            self.go(5, b["sum"][1], b["right"][1], ring.left)

    def end(self, part):
        b = self.bufs
        for k in ((3, 4), (2, 5))[part]:
            self.copies[k].wait_recv()
        return add(self.exact(self.ring.here, part)[...], b["left"][part][...], b["right"][part][...])


class Spread:
    def __init__(self, ring, slot, send, recv, out):
        self.ring, self.slot = ring, slot
        self.send, self.recv, self.out = send, recv, out
        self.copies = {}

    def go(self, k, ref, dev):
        self.copies[k] = self.out.go(ref, ref, self.send.at[k], self.recv.at[k], dev)

    def begin(self):
        ring, slot = self.ring, self.slot
        self.go(0, slot(ring.here, 0), ring.right)
        self.go(1, slot(ring.here, 1), ring.left)
        self.go(2, slot(ring.here, 1), ring.right)
        self.go(3, slot(ring.here, 0), ring.left)

    def middle(self, part):
        ring, slot = self.ring, self.slot
        self.copies[part].wait_recv()
        if part == 0:
            self.go(4, slot(ring.prev, 0), ring.right)
        else:
            self.go(5, slot(ring.next, 1), ring.left)

    def end(self):
        for k in range(2, 6):
            self.copies[k].wait_recv()


def activation(gate, up_value, hidden_grad):
    s = jax.nn.sigmoid(gate)
    hidden = (gate * s * up_value).astype(BF16)
    gate_grad = (hidden_grad * up_value * s * (1.0 + gate * (1.0 - s))).astype(BF16)
    up_grad = (hidden_grad * gate * s).astype(BF16)
    return hidden, gate_grad, up_grad


def lanes(chain, part):
    start, size = PARTS[chain][part]
    return pl.ds(start, size)


def scratch_plan():
    plan = {
        "x_all": pltpu.VMEM((2, 8, T, W), BF16),
        "c_all": pltpu.VMEM((2, 8, T, W), BF16),
        "sq_buf": pltpu.VMEM((16, 1, 128), F32),
        "inv_buf": pltpu.VMEM((16, 1, 128), F32),
        "dot_buf": pltpu.VMEM((16, 1, 128), F32),
        "gain_buf": pltpu.VMEM((16, 1, W), F32),
        "square": pltpu.VMEM((128, 128), F32),
        "inv_cols": pltpu.VMEM((128, 128), F32),
        "inv_own": pltpu.VMEM((128, 128), F32),
        "w_gu": pltpu.VMEM((W, 2 * U), BF16),
        "w_d": pltpu.VMEM((U, W), BF16),
        "grad_sum": pltpu.VMEM((T, W), F32),
    }
    for c, (_, t) in enumerate(CHUNKS):
        plan[f"nx{c}"] = pltpu.VMEM((16 * t, W), BF16)
        plan[f"pf{c}"] = pltpu.VMEM((4, 4, t, LANES), F32)
        plan[f"pb{c}"] = pltpu.VMEM((4, 4, t, LANES), BF16)
        plan[f"q{c}"] = pltpu.VMEM((4, 4, t, LANES), BF16)
        plan[f"total{c}"] = pltpu.VMEM((t, LANES), F32)
        plan[f"zf{c}"] = pltpu.VMEM((2, 2, 8, t, W), F32)
        plan[f"zb{c}"] = pltpu.VMEM((2, 2, 8, t, W), BF16)
        plan[f"pair{c}"] = pltpu.VMEM((2, 8, t, W), BF16)
        plan[f"go{c}"] = pltpu.VMEM((2, 4, 2, t, W), BF16)
        plan[f"come{c}"] = pltpu.VMEM((2, 4, 2, t, W), BF16)
        for chain in range(2):
            for part in range(2):
                size = PARTS[chain][part][1]
                plan[f"mf{c}{chain}{part}"] = pltpu.VMEM((4, t, size), F32)
                plan[f"mb{c}{chain}{part}"] = pltpu.VMEM((4, t, size), BF16)
                for name in ("hop", "sum", "left", "right"):
                    plan[f"big_{name}{c}{chain}{part}"] = pltpu.VMEM((4, t, size), BF16)
                    plan[f"small_{name}{c}{chain}{part}"] = pltpu.VMEM((t, size), BF16)
    n = len(CHUNKS)
    for name, shape in (
        ("row", (n, 2, 4, 6)), ("ring", (2, 4, 2)), ("mate", (8, 2)), ("sq", (15,)), ("inv", (15,)),
        ("pairs", (n, 2)), ("zring", (n, 2, 4, 2)), ("dot", (15,)), ("gain", (15,)),
    ):
        plan[name + "_send"] = pltpu.SemaphoreType.DMA(shape)
        plan[name + "_recv"] = pltpu.SemaphoreType.DMA(shape)
    return plan


PLAN = scratch_plan()


def kernel(
    tok, cot, gain, gate_w, up_w, down_w, keep_gu, keep_d,
    branch_out, tokens_out, gain_out, gu_out, d_out, *scratch,
):
    s = dict(zip(PLAN, scratch))
    dp, row, z = lax.axis_index("dp"), lax.axis_index("row"), lax.axis_index("col")
    me = dp * 8 + z
    px, py = row // 4, lax.rem(row, 4)
    row_peers, col_peers = peers_of_row(row), peers_of_cols(dp, z)
    right, left = {"col": lax.rem(z + 1, 8)}, {"col": lax.rem(z + 7, 8)}
    mate = {"dp": 1 - dp}
    out = Sender()
    x_all, c_all = s["x_all"], s["c_all"]
    square = s["square"]

    def as_row(column):
        square[...] = jnp.zeros((128, 128), F32)
        square[pl.ds(0, T), :] = jnp.broadcast_to(column, (T, 128))
        return jnp.transpose(square[...])[0:1]

    token_f = tok[...].astype(F32)
    x_all[dp, z] = tok[...]
    c_all[dp, z] = cot[...]
    s["sq_buf"][row] = as_row(jnp.sum(token_f * token_f, axis=1, keepdims=True))
    greet(row_peers + col_peers)

    alls = (x_all, c_all)

    def ring(side, step, unit):
        block = lax.rem(z + (9 - step if side == 0 else step + 7), 8)
        here = (tok, cot)[unit] if step == 1 else alls[unit].at[dp, block]
        return out.go(
            here, alls[unit].at[dp, block], s["ring_send"].at[side, step - 1, unit],
            s["ring_recv"].at[side, step - 1, unit], right if side == 0 else left,
        )

    def pair(slot, block, unit, own=False):
        here = (tok, cot)[unit] if own else alls[unit].at[dp, block]
        return out.go(
            here, alls[unit].at[dp, block], s["mate_send"].at[slot, unit], s["mate_recv"].at[slot, unit], mate
        )

    flying, mated = {}, []
    for unit in range(2):
        for side in range(2):
            u = unit if side == 0 else 1 - unit
            flying[side, 1, u] = ring(side, 1, u)
    squared = [
        out.go(
            s["sq_buf"].at[row], s["sq_buf"].at[row], s["sq_send"].at[k], s["sq_recv"].at[k], row_peers[k]
        )
        for k in range(15)
    ]
    for unit in range(2):
        mated.append(pair(0, z, unit, own=True))

    def mask_rows(i):
        rows = pl.ds(pl.multiple_of(i * 128, 128), 128)
        for j in range(14):
            piece = (gate_w, up_w)[j // 7][rows, pl.ds((j % 7) * 128, 128)]
            s["w_gu"][rows, pl.ds(j * 128, 128)] = (piece.astype(F32) * keep_gu[i, j].astype(F32)).astype(BF16)

    def mask_down(i):
        rows = pl.ds(pl.multiple_of(i * 128, 128), 128)
        for j in range(4):
            piece = down_w[rows, pl.ds(j * 128, 128)]
            s["w_d"][rows, pl.ds(j * 128, 128)] = (piece.astype(F32) * keep_d[i, j].astype(F32)).astype(BF16)

    inv_done = []
    for step in range(1, 5):
        for unit in range(2):
            for side in range(2):
                u = unit if side == 0 else 1 - unit
                if step == 4 and u != side:
                    continue
                flying[side, step, u].wait_recv()
                if step < 3 or (step == 3 and u == side):
                    flying[side, step + 1, u] = ring(side, step + 1, u)
                block = lax.rem(z + (8 - step if side == 0 else step), 8)
                mated.append(pair(step if side == 0 or step == 4 else step + 4, block, u))
        if step == 1:
            for copy in squared:
                copy.wait_recv()
            total = s["sq_buf"][0]
            for k in range(1, 16):
                total = total + s["sq_buf"][k]
            inv_row = lax.rsqrt(total / D + 1e-05)
            s["inv_buf"][me] = inv_row
            at = s["inv_buf"].at[me]
            inv_done = [
                out.go(at, at, s["inv_send"].at[k], s["inv_recv"].at[k], col_peers[k]) for k in range(15)
            ]
            s["inv_own"][...] = jnp.transpose(jnp.broadcast_to(inv_row, (128, 128)))
        if step == 2:
            @pl.loop(0, 4)
            def _(i):
                mask_rows(i)
        if step == 3:
            @pl.loop(0, 7)
            def _(i):
                mask_down(i)
    for copy in inv_done:
        copy.wait_recv()
    square[...] = jnp.zeros((128, 128), F32)
    for b in range(16):
        square[pl.ds(b, 1), :] = s["inv_buf"][b]
    s["inv_cols"][...] = jnp.transpose(square[...])
    for copy in mated:
        copy.wait_recv()

    def at(x, y):
        return {"row": x * 4 + y}

    rings = (
        Ring(px, at(lax.rem(px + 1, 4), py), at(lax.rem(px + 3, 4), py)),
        Ring(py, at(px, lax.rem(py + 1, 4)), at(px, lax.rem(py + 3, 4))),
    )

    def pieces(ref, chain):
        if chain == 0:
            return lambda d, part: ref.at[d, :, :, lanes(chain, part)]
        return lambda d, part: ref.at[:, d, :, lanes(chain, part)]

    def project(c):
        r0, t = CHUNKS[c]
        nx, pf, pb = s[f"nx{c}"], s[f"pf{c}"], s[f"pb{c}"]
        for b in range(16):
            value = x_all[b // 8, b % 8, pl.ds(r0, t), :].astype(F32)
            inv = s["inv_cols"][pl.ds(r0, t), b : b + 1]
            nx[pl.ds(b * t, t), :] = (value * inv * gain[...]).astype(BF16)

        @pl.loop(0, 7)
        def _(j):
            wide = pl.ds(pl.multiple_of(j * 256, 256), 256)
            value = jnp.dot(nx[...], s["w_gu"][:, wide], preferred_element_type=F32).reshape(4, 4, t, 256)
            pf[:, :, :, wide] = value
            pb[:, :, :, wide] = value.astype(BF16)
            seen = c_all[:, :, pl.ds(r0, t), :].reshape(16 * t, W)
            rows = pl.ds(pl.multiple_of(j * 128, 128), 128)
            value = lax.dot_general(seen, s["w_d"][rows, :], LAST, preferred_element_type=F32)
            value = value.reshape(4, 4, t, 128)
            narrow = pl.ds(pl.multiple_of(2 * U + j * 128, 128), 128)
            pf[:, :, :, narrow] = value
            pb[:, :, :, narrow] = value.astype(BF16)

    def flow(c):
        r0, t = CHUNKS[c]
        q, total = s[f"q{c}"], s[f"total{c}"]

        def bufs(size, chain):
            return {
                name: [s[f"{size}_{name}{c}{chain}{part}"] for part in range(2)]
                for name in ("hop", "sum", "left", "right")
            }

        def sems(chain, stage):
            return s["row_send"].at[c, chain, stage], s["row_recv"].at[c, chain, stage]

        project(c)
        one = [
            Scatter(
                rings[k], pieces(s[f"pb{c}"], k), pieces(s[f"pf{c}"], k), bufs("big", k), *sems(k, 0), out
            )
            for k in range(2)
        ]
        for k in range(2):
            one[k].begin()
        yield
        for part in range(2):
            for k in range(2):
                one[k].middle(part)
        yield
        two = []
        for k in range(2):
            exact = [s[f"mf{c}{k}{part}"] for part in range(2)]
            wire = [s[f"mb{c}{k}{part}"] for part in range(2)]
            for part in range(2):
                value = one[k].end(part)
                exact[part][...] = value
                wire[part][...] = value.astype(BF16)
            two.append(
                Scatter(
                    rings[1 - k], lambda d, part, wire=wire: wire[part].at[d],
                    lambda d, part, exact=exact: exact[part].at[d], bufs("small", k), *sems(k, 1), out,
                )
            )
            two[k].begin()
        yield
        for part in range(2):
            for k in range(2):
                two[k].middle(part)
        yield
        for k in range(2):
            for part in range(2):
                total[:, lanes(k, part)] = two[k].end(part)
        values = activation(total[:, pl.ds(0, U)], total[:, pl.ds(U, U)], total[:, pl.ds(2 * U, U)])
        for i in range(3):
            q[px, py, :, pl.ds(i * U, U)] = values[i]

        def near(k):
            if k == 0:
                return lambda d, part: q.at[px, d, :, lanes(k, part)]
            return lambda d, part: q.at[d, py, :, lanes(k, part)]

        three = [Spread(rings[1 - k], near(k), *sems(k, 2), out) for k in range(2)]
        four = [Spread(rings[k], pieces(q, k), *sems(k, 3), out) for k in range(2)]
        for k in range(2):
            three[k].begin()
        yield
        for part in range(2):
            for k in range(2):
                three[k].middle(part)
        yield
        for k in range(2):
            three[k].end()
            four[k].begin()
        yield
        for part in range(2):
            for k in range(2):
                four[k].middle(part)
        yield
        for k in range(2):
            four[k].end()

        zf, zb, pair_buf = s[f"zf{c}"], s[f"zb{c}"], s[f"pair{c}"]
        go_buf, come_buf = s[f"go{c}"], s[f"come{c}"]
        paired = []
        for unit in range(2):
            @pl.loop(0, 4)
            def _(j, unit=unit):
                part = pl.ds(pl.multiple_of(j * 128, 128), 128)
                if unit == 0:
                    seen = q[:, :, :, pl.ds(0, U)].reshape(16 * t, U)
                    value = jnp.dot(seen, s["w_d"][:, part], preferred_element_type=F32)
                else:
                    seen = q[:, :, :, pl.ds(U, 2 * U)].reshape(16 * t, 2 * U)
                    value = lax.dot_general(seen, s["w_gu"][part, :], LAST, preferred_element_type=F32)
                value = value.reshape(2, 8, t, 128)
                zf[unit, :, :, :, part] = value
                zb[unit, :, :, :, part] = value.astype(BF16)

            paired.append(
                out.go(
                    zb.at[unit, 1 - dp], pair_buf.at[unit], s["pairs_send"].at[c, unit],
                    s["pairs_recv"].at[c, unit], mate,
                )
            )
        yield

        def mine(off, unit):
            dest = lax.rem(z + off, 8)
            return add(zf[unit, dp, dest], pair_buf[unit, dest])

        for copy in paired:
            copy.wait_recv()
        hops = {}
        for step in range(1, 5):
            for unit in range(2):
                for side in range(2):
                    u = unit if side == 0 else 1 - unit
                    if step == 1 and u != side:
                        continue
                    value = mine(5 - step if side == 0 else 3 + step, u)
                    if step > 2 or (step == 2 and u == side):
                        hops[side, step - 1, u].wait_recv()
                        value = value + come_buf[side, step - 2, u].astype(F32)
                    go_buf[side, step - 1, u] = value.astype(BF16)
                    hops[side, step, u] = out.go(
                        go_buf.at[side, step - 1, u], come_buf.at[side, step - 1, u],
                        s["zring_send"].at[c, side, step - 1, u], s["zring_recv"].at[c, side, step - 1, u],
                        right if side == 0 else left,
                    )
            yield
        for unit in range(2):
            value = mine(0, unit)
            for side in range(2):
                hops[side, 4, unit].wait_recv()
                value = value + come_buf[side, 3, unit].astype(F32)
            if unit == 0:
                branch_out[pl.ds(r0, t), :] = value.astype(BF16)
            else:
                s["grad_sum"][pl.ds(r0, t), :] = value

    def weight_grads():
        for start, size in ((0, 4), (4, 3)):
            @pl.loop(start, start + size)
            def _(j):
                wide = pl.ds(pl.multiple_of(j * 256, 256), 256)
                from_q = pl.ds(pl.multiple_of(U + j * 256, 128), 256)
                value = jnp.zeros((W, 256), F32)
                for c, (_, t) in enumerate(CHUNKS):
                    value = value + lax.dot_general(
                        s[f"nx{c}"][...], s[f"q{c}"][:, :, :, from_q].reshape(16 * t, 256), FIRST,
                        preferred_element_type=F32,
                    )
                for i in range(4):
                    for h in range(2):
                        gu_out[pl.ds(i * 128, 128), pl.ds(pl.multiple_of(j * 256 + h * 128, 128), 128)] = (
                            value[i * 128 : i * 128 + 128, h * 128 : h * 128 + 128]
                            * keep_gu[i, 2 * j + h].astype(F32)
                        )
            yield

        @pl.loop(0, 7)
        def _(j):
            rows = pl.ds(pl.multiple_of(j * 128, 128), 128)
            value = jnp.zeros((128, W), F32)
            for c, (r0, t) in enumerate(CHUNKS):
                value = value + lax.dot_general(
                    s[f"q{c}"][:, :, :, rows].reshape(16 * t, 128),
                    c_all[:, :, pl.ds(r0, t), :].reshape(16 * t, W), FIRST, preferred_element_type=F32,
                )
            for i in range(4):
                d_out[rows, pl.ds(i * 128, 128)] = value[:, i * 128 : i * 128 + 128] * keep_d[j, i].astype(F32)
        yield

    n = len(CHUNKS)
    flows = [flow(c) for c in range(n)]
    grads = weight_grads()
    live = set(range(n))
    slot = 0
    while live:
        for c in range(n):
            if c in live and slot >= SKEW * c:
                try:
                    next(flows[c])
                except StopIteration:
                    live.discard(c)
        if slot >= SKEW * (n - 1) + 9:
            next(grads, None)
        slot += 1
    for _ in grads:
        pass

    normed_grad = s["grad_sum"][...]
    token_f = tok[...].astype(F32)
    inv_rms = s["inv_own"][pl.ds(0, T), 0:1]
    weighted = normed_grad * token_f
    s["gain_buf"][me] = jnp.sum(weighted * inv_rms, axis=0, keepdims=True)
    s["dot_buf"][row] = as_row(jnp.sum(gain[...] * weighted, axis=1, keepdims=True))
    small = []
    for k in range(15):
        at_row, at_me = s["dot_buf"].at[row], s["gain_buf"].at[me]
        small.append(out.go(at_row, at_row, s["dot_send"].at[k], s["dot_recv"].at[k], row_peers[k]))
        small.append(out.go(at_me, at_me, s["gain_send"].at[k], s["gain_recv"].at[k], col_peers[k]))
    for copy in small:
        copy.wait_recv()
    inner, gain_total = s["dot_buf"][0], s["gain_buf"][0]
    for k in range(1, 16):
        inner = inner + s["dot_buf"][k]
        gain_total = gain_total + s["gain_buf"][k]
    gain_out[...] = gain_total
    square[...] = jnp.transpose(jnp.broadcast_to(inner, (128, 128)))
    inner_col = square[pl.ds(0, T), 0:1]
    tokens_out[...] = inv_rms * gain[...] * normed_grad - token_f * inv_rms * inv_rms * inv_rms * inner_col / D
    out.drain()


def on_device(
    tokens, norm_gain, gate_weight, up_weight, down_weight, gate_keep, up_keep, down_keep, cotangent
):
    branch, grad_tokens, grad_gain, grad_gu, grad_down = pl.pallas_call(
        kernel,
        out_shape=(
            jax.ShapeDtypeStruct((T, W), BF16),
            jax.ShapeDtypeStruct((T, W), F32),
            jax.ShapeDtypeStruct((1, W), F32),
            jax.ShapeDtypeStruct((W, 2 * U), F32),
            jax.ShapeDtypeStruct((U, W), F32),
        ),
        in_specs=[VM] * 6 + [SM] * 2,
        out_specs=(VM,) * 5,
        scratch_shapes=list(PLAN.values()),
        compiler_params=pltpu.CompilerParams(
            collective_id=0, has_side_effects=True, vmem_limit_bytes=60 * 1024 * 1024
        ),
        name="feed_forward",
    )(
        tokens, cotangent, norm_gain[None, :], gate_weight, up_weight, down_weight,
        jnp.concatenate([gate_keep, up_keep], axis=1), down_keep,
    )
    return branch, grad_tokens, grad_gain[0], grad_gu[:, :U], grad_gu[:, U:], grad_down


def solution(mesh):
    wide = P("row", ("dp", "col"))
    tall = P(("dp", "col"), "row")
    return jax.shard_map(
        on_device,
        mesh=mesh,
        in_specs=(tall, P("row"), wide, wide, tall, wide, wide, tall, tall),
        out_specs=(tall, tall, P("row"), wide, wide, tall),
        check_vma=False,
    )
```
